32 devices in a mesh: dp: 4 (over z), ctx: 2 (over core), tensor: 4 (over y, x).
Axes of the slice: x: 2, y: 2, z: 4, core: 2. Of those that a mesh axis runs over, the one named last changes fastest.
Arguments:
- tokens: bfloat16 [4, 1024, 2048], P('dp', 'ctx', 'tensor'), may hold values from -6 to 6
- norm_gain: bfloat16 [2048], P('tensor'), may hold values from 0.5 to 1.5
- inner_weight: bfloat16 [2048, 4096], P(('dp', 'ctx'), 'tensor'), may hold values from -0.125 to 0.125
- gate_weight: bfloat16 [2048, 4096], P(('dp', 'ctx'), 'tensor'), may hold values from -0.125 to 0.125
- conv_weight: float32 [4, 4096], P(None, 'tensor'), may hold values from -3 to 3
- conv_bias: float32 [4096], P('tensor'), may hold values from -3 to 3
- select_weight: bfloat16 [160, 4096], P(('dp', 'ctx'), 'tensor'), may hold values from -0.09375 to 0.09375
- step_weight: bfloat16 [128, 4096], P(('dp', 'ctx'), 'tensor'), may hold values from -0.5 to 0.5
- step_bias: float32 [4096], P('tensor'), may hold values from -7 to -2.5
- log_decay: float32 [16, 4096], P(None, 'tensor'), may hold values from 0 to 2.77
- skip_gain: float32 [4096], P('tensor'), may hold values from 0.5 to 1.5
- out_weight: bfloat16 [4096, 2048], P('tensor', ('dp', 'ctx')), may hold values from -0.1875 to 0.1875
- cotangent: bfloat16 [4, 1024, 2048], P('dp', 'ctx', 'tensor'), may hold values from -6 to 6
Outputs:
- layer_out: float32 [4, 1024, 2048], P('dp', 'ctx', 'tensor')
- tokens_grad: float32 [4, 1024, 2048], P('dp', 'ctx', 'tensor')
- gain_grad: float32 [2048], P('tensor')
- inner_weight_grad: float32 [2048, 4096], P(('dp', 'ctx'), 'tensor')
- gate_weight_grad: float32 [2048, 4096], P(('dp', 'ctx'), 'tensor')
- conv_weight_grad: float32 [4, 4096], P(None, 'tensor')
- conv_bias_grad: float32 [4096], P('tensor')
- select_weight_grad: float32 [160, 4096], P(('dp', 'ctx'), 'tensor')
- step_weight_grad: float32 [128, 4096], P(('dp', 'ctx'), 'tensor')
- step_bias_grad: float32 [4096], P('tensor')
- log_decay_grad: float32 [16, 4096], P(None, 'tensor')
- skip_gain_grad: float32 [4096], P('tensor')
- out_weight_grad: float32 [4096, 2048], P('tensor', ('dp', 'ctx'))
The draws below stay inside these ranges and needn't reach their ends.
All inputs are finite; a program needn't handle non-finite values.
Results may differ from the reference program's by a relative error of at most 0.012.
Values may be sent and summed in bfloat16 or wider, within the bound.
No kernel may reach another device: no remote copies, remote signals or barrier semaphores. Data moves between devices by JAX's collectives and lax.ppermute only.
A program may use at most 512 MiB of HBM per device.

```python
import math
import jax
import jax.numpy as jnp
from jax import lax

D = 2048
INNER = 4096
STATE = 16
KCONV = 4
DT_RANK = 128
LENGTH = 1024
BLOCK = 256
SEQS = 4


def shard_levels(rng, extent, cuts, least, top_value):
    loudness = 1.0
    for dim, blocks in cuts:
        draws = jax.random.uniform(jax.random.fold_in(jax.random.fold_in(rng, 6), dim), (blocks,), jnp.float32, least / len(cuts), top_value / len(cuts))
        loudness = loudness * jnp.repeat(jnp.exp(draws), extent[dim] // blocks).reshape((-1,) + (1,) * (len(extent) - 1 - dim))
    return loudness


def scatter_about(own_key, dims, width, limit, shards=(), kind=jnp.bfloat16):
    loudness = shard_levels(own_key, dims, shards, -0.22, 0.18) if shards else 1.0
    values = jax.random.normal(own_key, dims, jnp.float32) * width * loudness
    return jnp.minimum(jnp.maximum(values, -limit), limit).astype(kind)


def setup_inputs(seed: int = 0) -> dict:
    splits = jax.random.split(jax.random.key(seed), 14)
    tokens = scatter_about(splits[0], (SEQS, LENGTH, D), 1.0, 6.0, ((0, 4), (1, 2), (2, 4)))
    norm_gain = jnp.clip(1.0 + 0.1 * jax.random.normal(splits[1], (D,), jnp.float32), 0.5, 1.5).astype(jnp.bfloat16)
    inner_weight = scatter_about(splits[2], (D, INNER), D ** -0.5, 0.125, ((0, 8), (1, 4)))
    gate_weight = scatter_about(splits[3], (D, INNER), D ** -0.5, 0.125, ((0, 8), (1, 4)))
    conv_weight = scatter_about(splits[4], (KCONV, INNER), KCONV ** -0.5, 3.0, ((1, 4),), jnp.float32)
    conv_bias = scatter_about(splits[5], (INNER,), 0.5, 3.0, ((0, 4),), jnp.float32)
    select_weight = scatter_about(splits[6], (DT_RANK + 2 * STATE, INNER), INNER ** -0.5, 0.09375, ((0, 8), (1, 4)))
    step_weight = scatter_about(splits[7], (DT_RANK, INNER), DT_RANK ** -0.5, 0.5, ((0, 8), (1, 4)))
    step_bias = jnp.clip(-7.0 + 4.5 * jax.random.uniform(splits[8], (INNER,), jnp.float32) ** shard_levels(splits[8], (INNER,), ((0, 4),), -0.2, 0.2), -7.0, -2.5)
    log_decay = jnp.clip(2.77 * jax.random.uniform(splits[9], (STATE, INNER), jnp.float32) ** shard_levels(splits[9], (STATE, INNER), ((1, 4),), -0.2, 0.2), 0.0, 2.77)
    skip_gain = jnp.clip(1.0 + 0.1 * jax.random.normal(splits[10], (INNER,), jnp.float32), 0.5, 1.5)
    out_weight = scatter_about(splits[11], (INNER, D), (INNER // 4) ** -0.5, 0.1875, ((0, 4), (1, 8)))
    cotangent = scatter_about(splits[12], (SEQS, LENGTH, D), 1.0, 6.0, ((0, 4), (1, 2), (2, 4)))
    return dict(tokens=tokens, norm_gain=norm_gain, inner_weight=inner_weight, gate_weight=gate_weight, conv_weight=conv_weight, conv_bias=conv_bias, select_weight=select_weight, step_weight=step_weight, step_bias=step_bias, log_decay=log_decay, skip_gain=skip_gain, out_weight=out_weight, cotangent=cotangent)


EPS = 1e-05

@jax.custom_vjp
def low(v):
    return lax.optimization_barrier(v.astype(jnp.bfloat16)).astype(jnp.float32)

@jax.custom_vjp
def low_back(v):
    return v

def low_keep(v):
    return (low(v), None)

def low_pass(kept, grad):
    return (grad,)

def back_keep(v):
    return (v, None)

def back_low(kept, grad):
    return (low(grad),)
low.defvjp(low_keep, low_pass)
low_back.defvjp(back_keep, back_low)

def product(operand, partner, pattern):
    return jnp.einsum(pattern, operand, partner, precision=lax.Precision.HIGHEST)

def scan_block(carried, pieces, decay_rate):

    def advance(current, one_token):
        step_delta, step_entry, step_read, step_conv = one_token
        current = jnp.exp(step_delta[:, None, :] * decay_rate[None]) * current + step_entry[:, :, None] * (step_delta * step_conv)[:, None, :]
        return (current, lax.optimization_barrier(jnp.sum(current * step_read[:, :, None], axis=1)))
    return lax.scan(advance, carried, pieces)

def forward(tokens, norm_gain, inner_weight, gate_weight, conv_weight, conv_bias, select_weight, step_weight, step_bias, log_decay, skip_gain, out_weight):
    seq_count = tokens.shape[0]
    inverse_rms = lax.rsqrt(lax.optimization_barrier(jnp.mean(tokens * tokens, axis=-1, keepdims=True)) + EPS)
    normed = low(tokens * inverse_rms * norm_gain)
    inner_act = low(low_back(product(normed, inner_weight, 'gtd,de->gte')))
    gate_act = low_back(product(normed, gate_weight, 'gtd,de->gte'))
    padded = jnp.pad(inner_act, ((0, 0), (KCONV - 1, 0), (0, 0)))
    conv_pre = conv_bias + conv_weight[0] * padded[:, 0:LENGTH]
    for offset in range(1, KCONV):
        conv_pre = conv_pre + conv_weight[offset] * padded[:, offset:offset + LENGTH]
    conv_out = low(jax.nn.silu(conv_pre))
    projected = low_back(product(conv_out, select_weight, 'gte,re->gtr'))
    step_in = low(projected[..., :DT_RANK])
    entry_map = projected[..., DT_RANK:DT_RANK + STATE]
    read_map = projected[..., DT_RANK + STATE:]
    step_size = jax.nn.softplus(low_back(product(step_in, step_weight, 'gtr,re->gte')) + step_bias)
    decay_rate = -jnp.exp(log_decay)
    blocks = LENGTH // BLOCK

    def to_blocks(values):
        return jnp.transpose(values.reshape(seq_count, blocks, BLOCK, values.shape[-1]), (1, 2, 0, 3))
    zero_state = jnp.zeros((seq_count, STATE, INNER), tokens.dtype)
    runner = jax.checkpoint(scan_block)

    def by_block(carried, pieces):
        return runner(carried, pieces, decay_rate)
    _, outputs = lax.scan(by_block, zero_state, (to_blocks(step_size), to_blocks(entry_map), to_blocks(read_map), to_blocks(conv_out)))
    scanned = jnp.transpose(outputs, (2, 0, 1, 3)).reshape(seq_count, LENGTH, INNER)
    scan_out = scanned + skip_gain * conv_out
    gated = low(scan_out * jax.nn.silu(gate_act))
    branch = low_back(product(gated, out_weight, 'gte,ed->gtd'))
    return tokens + branch

def reference(tokens, norm_gain, inner_weight, gate_weight, conv_weight, conv_bias, select_weight, step_weight, step_bias, log_decay, skip_gain, out_weight, cotangent):
    params = tuple((entry.astype(jnp.float32) for entry in (norm_gain, inner_weight, gate_weight, conv_weight, conv_bias, select_weight, step_weight, step_bias, log_decay, skip_gain, out_weight)))
    cluster = math.gcd(SEQS, 4)
    rounds = SEQS // cluster
    token_groups = tokens.astype(jnp.float32).reshape(rounds, cluster, LENGTH, D)
    cot_groups = cotangent.astype(jnp.float32).reshape(rounds, cluster, LENGTH, D)

    def visit(totals, paired):
        piece, piece_cot = paired
        result, pullback = jax.vjp(forward, piece, *params)
        grads = pullback(piece_cot)
        totals = tuple((total + update for total, update in zip(totals, grads[1:])))
        return (totals, (result, grads[0]))
    zeros_init = tuple((jnp.zeros_like(entry) for entry in params))
    totals, (layer_out, tokens_grad) = lax.scan(visit, zeros_init, (token_groups, cot_groups))
    return (layer_out.reshape(SEQS, LENGTH, D), tokens_grad.reshape(SEQS, LENGTH, D), totals[0], totals[1], totals[2], totals[3], totals[4], totals[5], totals[6], totals[7], totals[8], totals[9], totals[10])
```

```python
import functools

import jax
import jax.numpy as jnp
from jax import lax
from jax.experimental import pallas as pl
from jax.experimental.pallas import tpu as pltpu
from jax.sharding import PartitionSpec as P

EPS = 1e-05
LOG2E = 1.4426950408889634
LN2 = 0.6931471805599453
LANES = 128
SUB = 8
TIME_BLOCK = 128
F32 = jnp.float32
BF16 = jnp.bfloat16


def silu_slope(values):
    logistic = jax.nn.sigmoid(values)
    return logistic * (1.0 + values * (1.0 - logistic))


def contract(operand, partner):
    return lax.dot_general(
        operand, partner, (((0,), (0,)), ((), ())), preferred_element_type=F32
    )


def against(operand, partner):
    return lax.dot_general(
        operand, partner, (((1,), (1,)), ((), ())), preferred_element_type=F32
    )


def matmul(operand, partner):
    return jnp.dot(operand, partner, preferred_element_type=F32)


def swap(value, axis, offset):
    peers = lax.axis_size(axis)
    return lax.ppermute(value, axis, [(i, i ^ offset) for i in range(peers)])


def gather_pieces(value, axis):
    return [value] + [swap(value, axis, k) for k in range(1, lax.axis_size(axis))]


def stacked(pieces, axis):
    me = lax.axis_index(axis)
    out = jnp.zeros((len(pieces),) + pieces[0].shape, pieces[0].dtype)
    for k, piece in enumerate(pieces):
        out = lax.dynamic_update_slice_in_dim(out, piece[None], me ^ k, 0)
    return out


def exchange_sum(blocks_of, axis):
    me = lax.axis_index(axis)
    total = blocks_of(me).astype(F32)
    for k in range(1, lax.axis_size(axis)):
        total = total + swap(blocks_of(me ^ k), axis, k).astype(F32)
    return total


def everyone_sum(value, axis):
    total = value.astype(F32)
    for k in range(1, lax.axis_size(axis)):
        total = total + swap(value, axis, k).astype(F32)
    return total


def in_order(mine, other, position, axis):
    return jnp.where(
        position == 0,
        jnp.concatenate([mine, other], axis=axis),
        jnp.concatenate([other, mine], axis=axis),
    )


def half_of(value, which, axis):
    size = value.shape[axis] // 2
    return lax.dynamic_slice_in_dim(value, which * size, size, axis)


def assemble_kernel(count, order_ref, *refs):
    pieces, out_ref = refs[:count], refs[count]
    width = pieces[0].shape[1]
    for k in range(count):
        start = pl.multiple_of(order_ref[k] * width, LANES)
        out_ref[:, pl.ds(start, width)] = pieces[k][...]


def norm_kernel(count, total_width, order_ref, *refs):
    pieces, gains = refs[:count], refs[count : 2 * count]
    out_ref, inv_ref = refs[2 * count :]
    width = pieces[0].shape[1]
    total = None
    for k in range(count):
        part = pieces[k][...].astype(F32)
        squares = jnp.sum(part * part, axis=1, keepdims=True)
        total = squares if total is None else total + squares
    inverse = lax.rsqrt(total / total_width + EPS)
    inv_ref[...] = inverse
    for k in range(count):
        start = pl.multiple_of(order_ref[k] * width, LANES)
        normed = pieces[k][...].astype(F32) * inverse * gains[k][...].astype(F32)
        out_ref[:, pl.ds(start, width)] = normed.astype(BF16)


def row_block(rows):
    for size in (128, 64, 32, 16):
        if rows % size == 0:
            return size
    return rows


def assembled(pieces, order):
    rows, width = pieces[0].shape
    count = len(pieces)
    block = row_block(rows)
    return pl.pallas_call(
        functools.partial(assemble_kernel, count),
        grid_spec=pltpu.PrefetchScalarGridSpec(
            num_scalar_prefetch=1,
            grid=(rows // block,),
            in_specs=[pl.BlockSpec((block, width), lambda i, o: (i, 0))] * count,
            out_specs=pl.BlockSpec((block, width * count), lambda i, o: (i, 0)),
        ),
        out_shape=jax.ShapeDtypeStruct((rows, width * count), pieces[0].dtype),
        name="assemble",
    )(order, *pieces)


def normalized(pieces, gains, order):
    rows, width = pieces[0].shape
    count = len(pieces)
    block = row_block(rows)
    return pl.pallas_call(
        functools.partial(norm_kernel, count, float(width * count)),
        grid_spec=pltpu.PrefetchScalarGridSpec(
            num_scalar_prefetch=1,
            grid=(rows // block,),
            in_specs=[pl.BlockSpec((block, width), lambda i, o: (i, 0))] * count
            + [pl.BlockSpec((1, width), lambda i, o: (0, 0))] * count,
            out_specs=[
                pl.BlockSpec((block, width * count), lambda i, o: (i, 0)),
                pl.BlockSpec((block, 1), lambda i, o: (i, 0)),
            ],
        ),
        out_shape=[
            jax.ShapeDtypeStruct((rows, width * count), BF16),
            jax.ShapeDtypeStruct((rows, 1), F32),
        ],
        name="normalize",
    )(order, *pieces, *gains)


def row_of(ref, t, l):
    return ref[l, pl.ds(t, SUB, stride=0), :]


def spread(ref, values):
    for l in range(ref.shape[0]):
        ref[l] = values[:, l * LANES : (l + 1) * LANES]


def columns_of(values, j):
    return [
        jnp.broadcast_to(values[s : s + SUB, j : j + 1], (SUB, LANES))
        for s in range(0, values.shape[0], SUB)
    ]


def fold_rows(ref, count, l):
    total = ref[l, pl.ds(0, count, stride=SUB), :]
    for s in range(1, SUB):
        total = total + ref[l, pl.ds(s, count, stride=SUB), :]
    return total


def scan_kernel(
    dt_ref, x_ref, bt_ref, ct_ref, rate_ref, y_ref, start_ref, state, dt_rows, u_rows, part
):
    states, width = state.shape
    steps = dt_ref.shape[0]
    slices = [pl.ds(l, LANES) for l in range(0, width, LANES)]
    halves = [pl.ds(s, SUB) for s in range(0, states, SUB)]

    @pl.when(pl.program_id(0) == 0)
    def _():
        state[...] = jnp.zeros_like(state)

    start_ref[0] = state[...]
    spread(dt_rows, dt_ref[...])
    spread(u_rows, dt_ref[...] * x_ref[...].astype(F32))
    rates = [[rate_ref[h, l] for h in halves] for l in slices]

    def group(g, carried):
        base = pl.multiple_of(g * SUB, SUB)
        away = lax.rem(steps - base, steps)
        b_near = pltpu.roll(bt_ref[...], away, 1)
        c_near = pltpu.roll(ct_ref[...], away, 1)
        now = [list(one) for one in carried]
        for j in range(SUB):
            entry, read = columns_of(b_near, j), columns_of(c_near, j)
            row = pl.multiple_of((base + j) * SUB, SUB)
            for l, lanes in enumerate(slices):
                dt = row_of(dt_rows, base + j, l)
                u = row_of(u_rows, base + j, l)
                out = None
                for h in range(len(halves)):
                    new = jnp.exp2(dt * rates[l][h]) * now[l][h] + entry[h] * u
                    now[l][h] = new
                    term = read[h] * new
                    out = term if out is None else out + term
                part[l, pl.ds(row, SUB), :] = out
        return tuple(tuple(one) for one in now)

    first = tuple(tuple(state[h, l] for h in halves) for l in slices)
    last = lax.fori_loop(0, steps // SUB, group, first)
    for l, lanes in enumerate(slices):
        for h, rows in enumerate(halves):
            state[rows, lanes] = last[l][h]
        y_ref[:, lanes] = fold_rows(part, steps, l)


def scanned(dt, x, entry_t, read_t, rate):
    length, width = dt.shape
    states = rate.shape[0]
    block = TIME_BLOCK
    count = length // block
    groups = width // LANES
    by_time = pl.BlockSpec((block, width), lambda i: (i, 0))
    across = pl.BlockSpec((states, block), lambda i: (0, i))
    return pl.pallas_call(
        scan_kernel,
        grid=(count,),
        in_specs=[
            by_time,
            by_time,
            across,
            across,
            pl.BlockSpec((states, width), lambda i: (0, 0)),
        ],
        out_specs=[by_time, pl.BlockSpec((1, states, width), lambda i: (i, 0, 0))],
        out_shape=[
            jax.ShapeDtypeStruct((length, width), F32),
            jax.ShapeDtypeStruct((count, states, width), F32),
        ],
        scratch_shapes=[
            pltpu.VMEM((states, width), F32),
            pltpu.VMEM((groups, block, LANES), F32),
            pltpu.VMEM((groups, block, LANES), F32),
            pltpu.VMEM((groups, block * SUB, LANES), F32),
        ],
        name="scan_forward",
    )(dt, x, entry_t, read_t, rate)


def back_kernel(
    dt_ref,
    x_ref,
    grad_ref,
    bt_ref,
    ct_ref,
    rate_ref,
    start_ref,
    conv_ref,
    step_ref,
    entry_ref,
    read_ref,
    rate_grad_ref,
    ahead,
    dt_rows,
    u_rows,
    grad_rows,
    factors,
    levels,
    weighted,
    memory,
    entry_part,
    read_part,
):
    states, width = ahead.shape
    steps = dt_ref.shape[0]
    slices = [pl.ds(l, LANES) for l in range(0, width, LANES)]
    halves = [pl.ds(s, SUB) for s in range(0, states, SUB)]

    @pl.when(pl.program_id(0) == 0)
    def _():
        ahead[...] = jnp.zeros_like(ahead)
        rate_grad_ref[...] = jnp.zeros_like(rate_grad_ref)

    spread(dt_rows, dt_ref[...])
    spread(u_rows, dt_ref[...] * x_ref[...].astype(F32))
    spread(grad_rows, grad_ref[...])
    rates = [[rate_ref[h, l] for h in halves] for l in slices]
    levels[pl.ds(0, states), :] = start_ref[0]

    def rise(g, carried):
        base = pl.multiple_of(g * SUB, SUB)
        b_near = pltpu.roll(bt_ref[...], lax.rem(steps - base, steps), 1)
        now = [list(one) for one in carried]
        for j in range(SUB):
            entry = columns_of(b_near, j)
            row = pl.multiple_of((base + j) * states, states)
            for l, lanes in enumerate(slices):
                dt = row_of(dt_rows, base + j, l)
                u = row_of(u_rows, base + j, l)
                for h in range(len(halves)):
                    factor = jnp.exp2(dt * rates[l][h])
                    new = factor * now[l][h] + entry[h] * u
                    now[l][h] = new
                    factors[pl.ds(row + h * SUB, SUB), lanes] = factor
                    levels[pl.ds(row + states + h * SUB, SUB), lanes] = new
        return tuple(tuple(one) for one in now)

    first = tuple(tuple(start_ref[0, h, l] for h in halves) for l in slices)
    top = lax.fori_loop(0, steps // SUB, rise, first)

    def fall(k, carried):
        base = pl.multiple_of(steps - SUB - k * SUB, SUB)
        away = lax.rem(steps - base, steps)
        b_near = pltpu.roll(bt_ref[...], away, 1)
        c_near = pltpu.roll(ct_ref[...], away, 1)
        near, level, rate_sum = ([list(one) for one in part] for part in carried)
        for j in range(SUB - 1, -1, -1):
            entry, read = columns_of(b_near, j), columns_of(c_near, j)
            row = pl.multiple_of((base + j) * states, states)
            fold = pl.multiple_of((base + j) * SUB, SUB)
            to_entry, to_read = [None] * len(halves), [None] * len(halves)
            for l, lanes in enumerate(slices):
                dt = row_of(dt_rows, base + j, l)
                u = row_of(u_rows, base + j, l)
                grad = row_of(grad_rows, base + j, l)
                inward, recall = None, None
                for h in range(len(halves)):
                    adjoint = read[h] * grad + near[l][h]
                    passed = factors[pl.ds(row + h * SUB, SUB), lanes] * adjoint
                    before = levels[pl.ds(row + h * SUB, SUB), lanes]
                    kept = passed * before
                    rate_sum[l][h] = rate_sum[l][h] + kept * dt
                    one, two = adjoint * entry[h], kept * rates[l][h]
                    inward = one if inward is None else inward + one
                    recall = two if recall is None else recall + two
                    one, two = adjoint * u, level[l][h] * grad
                    to_entry[h] = one if to_entry[h] is None else to_entry[h] + one
                    to_read[h] = two if to_read[h] is None else to_read[h] + two
                    near[l][h] = passed
                    level[l][h] = before
                weighted[l, pl.ds(fold, SUB), :] = inward
                memory[l, pl.ds(fold, SUB), :] = recall
            for h in range(len(halves)):
                entry_part[pl.ds(row + h * SUB, SUB), :] = to_entry[h]
                read_part[pl.ds(row + h * SUB, SUB), :] = to_read[h]
        return tuple(tuple(tuple(one) for one in part) for part in (near, level, rate_sum))

    ahead_now = tuple(tuple(ahead[h, l] for h in halves) for l in slices)
    sums_now = tuple(tuple(rate_grad_ref[h, l] for h in halves) for l in slices)
    near, _, rate_sum = lax.fori_loop(0, steps // SUB, fall, (ahead_now, top, sums_now))
    for l, lanes in enumerate(slices):
        for h, rows in enumerate(halves):
            ahead[rows, lanes] = near[l][h]
            rate_grad_ref[rows, lanes] = rate_sum[l][h]
        inward = fold_rows(weighted, steps, l)
        conv_ref[:, lanes] = inward * dt_ref[:, lanes]
        step_ref[:, lanes] = inward * x_ref[:, lanes].astype(F32) + LN2 * fold_rows(
            memory, steps, l
        )
    ones = jnp.ones((SUB, LANES), F32)
    entry_ref[0] = against(ones, entry_part[...])
    read_ref[0] = against(ones, read_part[...])


def scanned_back(dt, x, grad, entry_t, read_t, rate, starts):
    length, width = dt.shape
    states = rate.shape[0]
    block = TIME_BLOCK
    count = length // block
    last = count - 1
    groups = width // LANES
    by_time = pl.BlockSpec((block, width), lambda i: (last - i, 0))
    across = pl.BlockSpec((states, block), lambda i: (0, last - i))
    fixed = pl.BlockSpec((states, width), lambda i: (0, 0))
    flat = pl.BlockSpec((1, SUB, block * states), lambda i: (last - i, 0, 0))
    conv, step, entry, read, rate_grad = pl.pallas_call(
        back_kernel,
        grid=(count,),
        in_specs=[
            by_time,
            by_time,
            by_time,
            across,
            across,
            fixed,
            pl.BlockSpec((1, states, width), lambda i: (last - i, 0, 0)),
        ],
        out_specs=[by_time, by_time, flat, flat, fixed],
        out_shape=[
            jax.ShapeDtypeStruct((length, width), F32),
            jax.ShapeDtypeStruct((length, width), F32),
            jax.ShapeDtypeStruct((count, SUB, block * states), F32),
            jax.ShapeDtypeStruct((count, SUB, block * states), F32),
            jax.ShapeDtypeStruct((states, width), F32),
        ],
        scratch_shapes=[
            pltpu.VMEM((states, width), F32),
            pltpu.VMEM((groups, block, LANES), F32),
            pltpu.VMEM((groups, block, LANES), F32),
            pltpu.VMEM((groups, block, LANES), F32),
            pltpu.VMEM((block * states, width), F32),
            pltpu.VMEM(((block + 1) * states, width), F32),
            pltpu.VMEM((groups, block * SUB, LANES), F32),
            pltpu.VMEM((groups, block * SUB, LANES), F32),
            pltpu.VMEM((block * states, LANES), F32),
            pltpu.VMEM((block * states, LANES), F32),
        ],
        name="scan_backward",
    )(dt, x, grad, entry_t, read_t, rate, starts)
    entry = entry[:, 0, :].reshape(length, states)
    read = read[:, 0, :].reshape(length, states)
    return conv, step, entry, read, rate_grad


def shards(
    tokens,
    norm_gain,
    inner_weight,
    gate_weight,
    conv_weight,
    conv_bias,
    select_weight,
    step_weight,
    step_bias,
    log_decay,
    skip_gain,
    out_weight,
    cotangent,
):
    local_len, part_width = tokens.shape[1:]
    core = lax.axis_index("ctx")
    seat = lax.axis_index("dp")
    place = lax.axis_index("tensor")
    peers = lax.axis_size("tensor")
    seats = lax.axis_size("dp")
    kernel = conv_weight.shape[0]
    states = log_decay.shape[0]
    half = conv_weight.shape[1] // 2
    order = place ^ jnp.arange(peers, dtype=jnp.int32)

    own_tokens = tokens[0]
    own_cot = cotangent[0]

    def core_rows(weight):
        other = swap(half_of(weight, 1 - core, 1), "ctx", 1)
        return in_order(half_of(weight, core, 1), other, core, 0)

    inner_rows, gate_rows, out_rows, select_rows, step_rows = (
        core_rows(weight)
        for weight in (inner_weight, gate_weight, out_weight.T, select_weight, step_weight)
    )

    def whole(rows):
        full = stacked(gather_pieces(rows, "dp"), "dp")
        return full.reshape((-1,) + rows.shape[1:])

    w_inner = whole(inner_rows)
    w_select = whole(select_rows)
    w_step = whole(step_rows)
    w_gate = whole(gate_rows)
    w_out = whole(out_rows)
    rank_width = w_step.shape[0]
    model_width = w_inner.shape[0]

    token_pieces = gather_pieces(own_tokens, "tensor")
    gain_pieces = gather_pieces(norm_gain[None], "tensor")
    normed_half, inverse_rms = normalized(token_pieces, gain_pieces, order)
    normed = in_order(normed_half, swap(normed_half, "ctx", 1), core, 0)
    cot_half = assembled(gather_pieces(own_cot, "tensor"), order)
    cot = in_order(cot_half, swap(cot_half, "ctx", 1), core, 0)
    length = normed.shape[0]

    own_conv_weight = half_of(conv_weight, core, 1)
    own_conv_bias = half_of(conv_bias, core, 0)
    own_step_bias = half_of(step_bias, core, 0)
    own_skip = half_of(skip_gain, core, 0)
    decay_rate = -jnp.exp(half_of(log_decay, core, 1))

    inner_act = matmul(normed, w_inner).astype(BF16)
    gate_act = matmul(normed, w_gate)
    extended = jnp.pad(inner_act, ((kernel - 1, 0), (0, 0))).astype(F32)
    conv_pre = own_conv_bias + own_conv_weight[0] * extended[0:length]
    for offset in range(1, kernel):
        conv_pre = conv_pre + own_conv_weight[offset] * extended[offset : offset + length]
    conv_low = jax.nn.silu(conv_pre).astype(BF16)

    def summed(terms):
        mine = half_of(terms, core, 0) + swap(half_of(terms, 1 - core, 0), "ctx", 1)
        total = everyone_sum(mine.astype(BF16), "tensor")
        return in_order(total, swap(total, "ctx", 1), core, 0)

    projected = summed(against(conv_low, w_select))
    step_in = projected[:, :rank_width].astype(BF16)
    maps_t = projected[:, rank_width:].T
    entry_t, read_t = maps_t[:states], maps_t[states:]
    step_arg = matmul(step_in, w_step) + own_step_bias
    step_size = jax.nn.softplus(step_arg)
    conv_wide = conv_low.astype(F32)
    rate2 = decay_rate * LOG2E

    local_out, starts = scanned(step_size, conv_low, entry_t, read_t, rate2)
    scan_out = local_out + own_skip * conv_wide
    gate_silu = jax.nn.silu(gate_act)
    gated = (scan_out * gate_silu).astype(BF16)

    def weight_sum(terms):
        rows = terms.shape[0] // seats
        terms = terms.astype(BF16)
        total = exchange_sum(
            lambda j: lax.dynamic_slice_in_dim(terms, j * rows, rows, 0), "dp"
        )
        other = swap(half_of(total, 1 - core, 0), "ctx", 1)
        return in_order(half_of(total, core, 0), other, core, 1)

    def feature_sum(terms):
        terms = terms.astype(BF16)
        mine = half_of(terms, core, 0).astype(F32) + swap(
            half_of(terms, 1 - core, 0), "ctx", 1
        ).astype(F32)
        mine = mine.astype(BF16)
        return exchange_sum(
            lambda j: lax.dynamic_slice_in_dim(mine, j * part_width, part_width, 1), "tensor"
        )

    out_weight_grad = weight_sum(contract(cot, gated)).T
    layer_out = own_tokens.astype(F32) + feature_sum(against(gated, w_out))

    gated_grad = matmul(cot, w_out)
    y_grad = gated_grad * gate_silu
    gate_low = (gated_grad * scan_out * silu_slope(gate_act)).astype(BF16)
    skip_local = jnp.sum(y_grad * conv_wide, axis=0)
    gate_weight_grad = weight_sum(contract(normed, gate_low))

    scan_conv_grad, step_grad, entry_grad, read_grad, rate_grad = scanned_back(
        step_size, conv_low, y_grad, entry_t, read_t, rate2, starts
    )
    step_arg_grad = step_grad * jax.nn.sigmoid(step_arg)
    step_bias_local = jnp.sum(step_arg_grad, axis=0)
    step_low = step_arg_grad.astype(BF16)
    step_weight_local = contract(step_in, step_low)
    proj_terms = jnp.concatenate([against(step_low, w_step), entry_grad, read_grad], axis=1)
    proj_grad = summed(proj_terms).astype(BF16)
    select_local = contract(proj_grad, conv_low)
    conv_out_grad = scan_conv_grad + y_grad * own_skip + matmul(proj_grad, w_select)
    conv_pre_grad = conv_out_grad * silu_slope(conv_pre)
    conv_bias_local = jnp.sum(conv_pre_grad, axis=0)
    conv_weight_local = [
        jnp.sum(conv_pre_grad * extended[offset : offset + length], axis=0)
        for offset in range(kernel)
    ]
    padded = jnp.pad(conv_pre_grad, ((0, kernel - 1), (0, 0)))
    inner_grad = own_conv_weight[0] * padded[kernel - 1 : kernel - 1 + length]
    for offset in range(1, kernel):
        begin = kernel - 1 - offset
        inner_grad = inner_grad + own_conv_weight[offset] * padded[begin : begin + length]
    inner_low = inner_grad.astype(BF16)
    inner_weight_grad = weight_sum(contract(normed, inner_low))
    select_weight_grad = weight_sum(select_local)
    step_weight_grad = weight_sum(step_weight_local)

    normed_terms = against(inner_low, w_inner) + against(gate_low, w_gate)
    normed_grad = feature_sum(normed_terms)
    own_x = own_tokens.astype(F32)
    own_gain = norm_gain.astype(F32)
    token_dots = everyone_sum(
        jnp.sum(normed_grad * own_gain * own_x, axis=-1)[None], "tensor"
    ).reshape(local_len, 1)
    cubed = inverse_rms * inverse_rms * inverse_rms
    tokens_grad = (
        own_cot.astype(F32)
        + inverse_rms * own_gain * normed_grad
        - own_x * cubed * token_dots / model_width
    )
    gain_local = jnp.sum(normed_grad * own_x * inverse_rms, axis=0)[None]
    gain_local = everyone_sum(gain_local, "dp")
    gain_grad = (gain_local + swap(gain_local, "ctx", 1))[0]

    rows = jnp.concatenate(
        [
            jnp.stack(conv_weight_local + [conv_bias_local, step_bias_local, skip_local]),
            rate_grad * decay_rate,
        ],
        axis=0,
    )
    rows = everyone_sum(rows, "dp")
    rows = in_order(rows, swap(rows, "ctx", 1), core, 1)
    return (
        layer_out[None],
        tokens_grad[None],
        gain_grad,
        inner_weight_grad,
        gate_weight_grad,
        rows[:kernel],
        rows[kernel],
        select_weight_grad,
        step_weight_grad,
        rows[kernel + 1],
        rows[kernel + 3 :],
        rows[kernel + 2],
        out_weight_grad,
    )


def solution(mesh):
    return jax.shard_map(
        shards,
        mesh=mesh,
        in_specs=(
            P("dp", "ctx", "tensor"),
            P("tensor"),
            P(("dp", "ctx"), "tensor"),
            P(("dp", "ctx"), "tensor"),
            P(None, "tensor"),
            P("tensor"),
            P(("dp", "ctx"), "tensor"),
            P(("dp", "ctx"), "tensor"),
            P("tensor"),
            P(None, "tensor"),
            P("tensor"),
            P("tensor", ("dp", "ctx")),
            P("dp", "ctx", "tensor"),
        ),
        out_specs=(
            P("dp", "ctx", "tensor"),
            P("dp", "ctx", "tensor"),
            P("tensor"),
            P(("dp", "ctx"), "tensor"),
            P(("dp", "ctx"), "tensor"),
            P(None, "tensor"),
            P("tensor"),
            P(("dp", "ctx"), "tensor"),
            P(("dp", "ctx"), "tensor"),
            P("tensor"),
            P(None, "tensor"),
            P("tensor"),
            P("tensor", ("dp", "ctx")),
        ),
        check_vma=False,
    )
```
